32 devices in a mesh: chan: 4 (over y, core), prof: 8 (over z, x).
Axes of the slice: x: 2, y: 2, z: 4, core: 2. Of those that a mesh axis runs over, the one named last changes fastest.
Arguments:
- observed: bfloat16 [32, 8448], P('prof', 'chan'), may hold values from -6 to 6
- eigvec: bfloat16 [8448, 300], P('chan'), may hold values from -0.0625 to 0.0625
- jacobian: bfloat16 [32, 8448, 400], P('prof', 'chan'), may hold values from -0.44921875 to 0.44921875
- radiance_base: bfloat16 [8448], P('chan'), may hold values from -1 to 1
- curvature: bfloat16 [8448], P('chan'), may hold values from -0.29882812 to 0.29882812
- block_mask: int32 [32, 256], P('prof', 'chan'), may hold values 0 or 1
- pc_weight: float32 [300], replicated, may hold values from 0.2 to 2
- prior_prec: float32 [400], replicated, may hold values from 0.3 to 3
- prior_mean: float32 [32, 400], P(('prof', 'chan')), may hold values from -6 to 6
- state0: float32 [32, 400], P(('prof', 'chan')), may hold values from -6 to 6
Outputs:
- states: float32 [32, 400], P(('prof', 'chan'))
The draws below stay inside these ranges and needn't reach their ends.
All inputs are finite; a program needn't handle non-finite values. No bound on the sum of `block_mask` on one device may be relied on, other than what follows from the above.
Results may differ from the reference program's by a relative error of at most 0.006.
Values may be sent and summed in bfloat16 or wider, within the bound.
A program may use at most 128 MiB of HBM per device.

```python
import math
import jax
import jax.numpy as jnp
from jax import lax

C = 8448
K = 300
S = 400
NBLK = 256
ITERS = 2
PROFILES = 32


def place_ends(values, key, smallest, top_value):
    longest = values.shape.index(max(values.shape))
    spots = []
    for shift in (0, 1):
        where = [jax.random.randint(jax.random.fold_in(key, axis), (), 0, length) for axis, length in enumerate(values.shape)]
        where[longest] = (where[longest] + shift) % values.shape[longest]
        spots.append(tuple(where))
    return values.at[spots[0]].set(smallest).at[spots[1]].set(top_value)


def block_scale(stream_key, extent, cuts, least, largest):
    gain, own = 1.0, jax.random.fold_in(stream_key, 6)
    for axis_at, blocks in cuts:
        steps = jnp.exp(jax.random.uniform(jax.random.fold_in(own, axis_at), (blocks,), jnp.float32, least / len(cuts), largest / len(cuts)))
        gain = gain * jnp.repeat(steps, extent[axis_at] // blocks).reshape([-1 if axis == axis_at else 1 for axis in range(len(extent))])
    return gain


def normal_values(own_key, shape, width, limit, shards=(), kind=jnp.bfloat16):
    level = block_scale(own_key, shape, shards, -0.22, 0.18) if shards else 1.0
    array = jax.random.normal(own_key, shape, jnp.float32) * width * level
    return jnp.minimum(jnp.maximum(array, -limit), limit).astype(kind)


def setup_inputs(seed: int = 0) -> dict:
    arg_keys = jax.random.split(jax.random.key(seed), 11)
    observed = normal_values(arg_keys[0], (PROFILES, C), 1.0, 6.0, ((0, 8), (1, 4)))
    eigvec = normal_values(arg_keys[1], (C, K), C ** -0.5, 0.0625, ((0, 4),))
    jacobian = normal_values(arg_keys[2], (PROFILES, C, S), 0.15, 0.44921875, ((0, 8), (1, 4)))
    radiance_base = jnp.clip(jax.random.uniform(arg_keys[3], (C,), jnp.float32, -1.0, 1.0) * block_scale(arg_keys[3], (C,), ((0, 4),), -0.4, 0.0), -1.0, 1.0).astype(jnp.bfloat16)
    curvature = jnp.clip(jax.random.uniform(arg_keys[4], (C,), jnp.float32, -0.29882812, 0.29882812) * block_scale(arg_keys[4], (C,), ((0, 4),), -0.4, 0.0), -0.29882812, 0.29882812).astype(jnp.bfloat16)
    block_mask = place_ends((jax.random.randint(arg_keys[5], (PROFILES, NBLK), 0, 4) < 3).astype(jnp.int32), jax.random.fold_in(arg_keys[5], 1), 0, 1)
    pc_weight = jnp.clip(jnp.exp(jax.random.uniform(arg_keys[6], (K,), jnp.float32, math.log(0.2), math.log(2.0))), 0.2, 2.0)
    prior_prec = jnp.clip(jnp.exp(jax.random.uniform(arg_keys[7], (S,), jnp.float32, math.log(0.3), math.log(3.0))), 0.3, 3.0)
    prior_mean = normal_values(arg_keys[8], (PROFILES, S), 1.0, 6.0, ((0, 32),), jnp.float32)
    state0 = normal_values(arg_keys[9], (PROFILES, S), 1.0, 6.0, ((0, 32),), jnp.float32)
    return dict(observed=observed, eigvec=eigvec, jacobian=jacobian, radiance_base=radiance_base, curvature=curvature, block_mask=block_mask, pc_weight=pc_weight, prior_prec=prior_prec, prior_mean=prior_mean, state0=state0)


def solve_step(states, pc_resid, pc_jacob, pc_weight, prior_prec, prior_mean):
    highest = lax.Precision.HIGHEST
    weighted_jac = pc_jacob * pc_weight[None, :, None]
    normal = jnp.einsum('rks,rkt->rst', weighted_jac, pc_jacob, precision=highest)
    normal = normal + jnp.eye(pc_jacob.shape[2], dtype=jnp.float32)[None] * prior_prec[None, None, :]
    gradient = jnp.einsum('rks,rk->rs', pc_jacob, pc_weight[None, :] * pc_resid, precision=highest)
    gradient = gradient + prior_prec[None, :] * (states - prior_mean)
    factor = jnp.linalg.cholesky(normal)

    def one_solve(fac, vec):
        return jax.scipy.linalg.cho_solve((fac, True), vec)
    update = jax.vmap(one_solve)(factor, gradient)
    return states - update

def reference(observed, eigvec, jacobian, radiance_base, curvature, block_mask, pc_weight, prior_prec, prior_mean, state0):
    block_width = C // NBLK
    valid_mask = jnp.repeat(block_mask.astype(jnp.float32), block_width, axis=1)
    shift_f = radiance_base.astype(jnp.float32)
    curve_f = curvature.astype(jnp.float32)
    eig_f = eigvec.astype(jnp.float32)
    highest = lax.Precision.HIGHEST
    blocks = 16
    count = PROFILES // blocks

    def retrieve(pieces):
        states, spectra, valid, pmean, jac_bf = pieces
        jac_f = jac_bf.astype(jnp.float32)
        for iteration in range(ITERS):
            state_bf = states.astype(jnp.bfloat16)
            linear = jnp.einsum('rs,rcs->rc', state_bf.astype(jnp.float32), jac_f, precision=highest)
            misfit = (valid * (shift_f + linear + 0.5 * curve_f * linear * linear - spectra.astype(jnp.float32))).astype(jnp.bfloat16)
            slope = valid * (1.0 + curve_f * linear)
            weighted = (slope[:, :, None] * eig_f[None]).astype(jnp.bfloat16)
            pc_resid = jnp.dot(misfit.astype(jnp.float32), eigvec.astype(jnp.float32), preferred_element_type=jnp.float32)
            pc_jacob = jnp.einsum('rck,rcs->rks', weighted.astype(jnp.float32), jac_f, precision=highest)
            states = solve_step(states, pc_resid, pc_jacob, pc_weight, prior_prec, pmean)
        return states
    shaped = (state0.reshape(count, blocks, S), observed.reshape(count, blocks, C), valid_mask.reshape(count, blocks, C), prior_mean.reshape(count, blocks, S), jacobian.reshape(count, blocks, C, S))
    result = lax.map(retrieve, shaped)
    return result.reshape(PROFILES, S)
```

```python
import functools
import jax, jax.numpy as jnp
from jax import lax
from jax.experimental import pallas as pl
from jax.experimental.pallas import tpu as pltpu

from jax.sharding import PartitionSpec as P

ITERS = 2
HI = lax.Precision.HIGHEST
TILE, LANES = 8, 128


def up(n, m):
    return -(-n // m) * m


def eliminate(mat, first, rows, width):
    tiles = rows // TILE
    spans = (width - first) // LANES
    sub = lax.broadcasted_iota(jnp.int32, (TILE, LANES), 0)

    def group(q, carry):
        base = pl.multiple_of(first + q * TILE, TILE)
        piv = [mat[pl.ds(base, TILE), first + w * LANES:first + (w + 1) * LANES] for w in range(spans)]

        def spread(tile, k):
            where = jnp.full((TILE, LANES), q * TILE + k, jnp.int32)
            return jnp.take_along_axis(tile, where, axis=1, mode="promise_in_bounds")

        cols = [spread(piv[0], k) for k in range(TILE)]
        for t in range(TILE):
            inv = 1.0 / jnp.broadcast_to(cols[t][t:t + 1], (TILE, LANES))
            at = sub == t
            factor = jnp.where(at, 1.0 - inv, cols[t] * inv)
            cols = [c if k <= t else c - factor * jnp.broadcast_to(c[t:t + 1], (TILE, LANES)) for k, c in enumerate(cols)]
            piv = [c - factor * jnp.broadcast_to(c[t:t + 1], (TILE, LANES)) for c in piv]
        lines = [[jnp.broadcast_to(c[k:k + 1], (TILE, LANES)) for k in range(TILE)] for c in piv]
        for i in range(tiles):
            at = slice(first + i * TILE, first + (i + 1) * TILE)
            old = [mat[at, first + w * LANES:first + (w + 1) * LANES] for w in range(spans)]
            mult = [spread(old[0], k) for k in range(TILE)]
            for w in range(spans):
                acc = [mult[k] * lines[w][k] for k in range(TILE)]
                while len(acc) > 1:
                    acc = [acc[2 * z] + acc[2 * z + 1] for z in range(len(acc) // 2)]
                mat[at, first + w * LANES:first + (w + 1) * LANES] = old[w] - acc[0]
        for w in range(spans):
            mat[pl.ds(base, TILE), first + w * LANES:first + (w + 1) * LANES] = piv[w]
        return carry

    lax.fori_loop(0, tiles, group, 0)


def solver_kernel(jac_ref, resid_ref, weight_ref, prec_ref, mean_ref, state_ref, out_ref, aug, mat, held):
    count, size = jac_ref.shape
    rows, lanes = mat.shape
    root = jnp.sqrt(prec_ref[...])
    aug[...] = jnp.zeros_like(aug)
    jac = jac_ref[...] * (1.0 / root)
    aug[0:count, :] = jac
    aug[rows:rows + 1, :] = (state_ref[...] - mean_ref[...]) * root
    full = lax.dot_general(aug[0:rows, :], aug[...], (((1,), (1,)), ((), ())), precision=HI, preferred_element_type=jnp.float32)
    r = lax.broadcasted_iota(jnp.int32, full.shape, 0)
    c = lax.broadcasted_iota(jnp.int32, full.shape, 1)
    mat[...] = full + jnp.where(r == c, 1.0 / weight_ref[...], 0.0) - jnp.where(c == rows, resid_ref[...], 0.0)
    for first in range(0, rows, LANES):
        here = min(LANES, rows - first)
        after = first + here
        if after < rows:
            held[0:here, 0:lanes - after] = mat[first:after, after:lanes]
        eliminate(mat, first, here, lanes)
        if after < rows:
            mat[after:rows, after:lanes] = mat[after:rows, after:lanes] - lax.dot_general(
                held[0:here, 0:rows - after], mat[first:after, after:lanes], (((0,), (0,)), ((), ())),
                precision=HI, preferred_element_type=jnp.float32)
    out_ref[...] = back(mat, aug, rows, lanes, mean_ref, root)


def back(mat, aug, rows, lanes, mean_ref, root):
    total = None
    solved = []
    start = (rows - 1) // LANES * LANES
    for first in range(start, -1, -LANES):
        here = min(LANES, rows - first)
        z = mat[first:first + here, rows:rows + 1]
        for at, width, later in solved:
            z = z - jnp.sum(mat[first:first + here, at:at + width] * later, axis=1, keepdims=True)
        part = jnp.sum(aug[first:first + here, :] * z, axis=0, keepdims=True)
        total = part if total is None else total + part
        if first > 0:
            flat = jnp.transpose(jnp.broadcast_to(z, (here, LANES)))[0:1, :]
            solved.append((first, here, flat))
    return mean_ref[...] + total / root


def solve(states, resid, jac, weight, prec, mean):
    count, size = jac.shape
    rows = up(count, TILE)
    lanes = up(rows + 1, LANES)
    wide = lanes
    weight = jnp.pad(weight, (0, rows - count), constant_values=1.0)[:, None]
    resid = jnp.pad(resid, ((0, rows - count), (0, 0)))
    vmem = pl.BlockSpec(memory_space=pltpu.VMEM)
    return pl.pallas_call(
        solver_kernel,
        out_shape=jax.ShapeDtypeStruct((1, size), jnp.float32),
        in_specs=[vmem] * 6,
        out_specs=vmem,
        scratch_shapes=[
            pltpu.VMEM((wide, size), jnp.float32),
            pltpu.VMEM((rows, lanes), jnp.float32),
            pltpu.VMEM((LANES, lanes), jnp.float32),
        ],
        compiler_params=pltpu.CompilerParams(vmem_limit_bytes=32 * 2**20),
    )(jac, resid, weight, prec[None, :], mean, states)


def project(state_bf, spectra, valid, eigvec, jacobian, radiance_base, curvature):
    shift_f = radiance_base.astype(jnp.float32)
    curve_f = curvature.astype(jnp.float32)
    linear = jnp.einsum("rs,rcs->rc", state_bf, jacobian, preferred_element_type=jnp.float32)
    misfit = (
        valid * (shift_f + linear + 0.5 * curve_f * linear * linear - spectra.astype(jnp.float32))
    ).astype(jnp.bfloat16)
    slope = valid * (1.0 + curve_f * linear)
    weighted = (slope[:, :, None] * eigvec[None]).astype(jnp.bfloat16)
    pc_resid = jnp.dot(misfit, eigvec, preferred_element_type=jnp.float32)
    pc_jacob = jnp.einsum("rck,rcs->rks", weighted, jacobian, preferred_element_type=jnp.float32)
    return (pc_resid, pc_jacob)


def local(
    observed,
    eigvec,
    jacobian,
    radiance_base,
    curvature,
    block_mask,
    pc_weight,
    prior_prec,
    prior_mean,
    state0,
):
    block_width = observed.shape[1] // block_mask.shape[1]
    states = state0
    valid = jnp.repeat(block_mask.astype(jnp.float32), block_width, axis=1)
    for iteration in range(ITERS):
        state_bf = lax.all_gather(states.astype(jnp.bfloat16), "chan", axis=0, tiled=True)
        pc_resid, pc_jacob = project(
            state_bf, observed, valid, eigvec, jacobian, radiance_base, curvature
        )
        pc_resid, pc_jacob = (
            lax.psum_scatter(pc_resid, "chan", scatter_dimension=0, tiled=True),
            lax.psum_scatter(pc_jacob, "chan", scatter_dimension=0, tiled=True),
        )
        own = [
            solve(states[p:p + 1], pc_resid[p][:, None], pc_jacob[p], pc_weight, prior_prec, prior_mean[p:p + 1])
            for p in range(states.shape[0])
        ]
        states = own[0] if len(own) == 1 else jnp.concatenate(own, axis=0)
    return states


def solution(mesh):
    return jax.shard_map(
        local,
        mesh=mesh,
        in_specs=(
            P("prof", "chan"),
            P("chan", None),
            P("prof", "chan", None),
            P("chan"),
            P("chan"),
            P("prof", "chan"),
            P(),
            P(),
            P(("prof", "chan"), None),
            P(("prof", "chan"), None),
        ),
        out_specs=P(("prof", "chan"), None),
        check_vma=False,
    )
```

```python
import functools
import jax, jax.numpy as jnp
from jax import lax
from jax.experimental import pallas as pl
from jax.experimental.pallas import tpu as pltpu

from jax.sharding import PartitionSpec as P

ITERS = 2
HI = lax.Precision.HIGHEST
TILE, LANES = 8, 128
MESH = pl.DeviceIdType.MESH


def up(n, m):
    return -(-n // m) * m


def eliminate(mat, first, rows, width):
    tiles = rows // TILE
    spans = (width - first) // LANES
    sub = lax.broadcasted_iota(jnp.int32, (TILE, LANES), 0)

    def group(q, carry):
        base = pl.multiple_of(first + q * TILE, TILE)
        piv = [mat[pl.ds(base, TILE), first + w * LANES:first + (w + 1) * LANES] for w in range(spans)]

        def spread(tile, k):
            where = jnp.full((TILE, LANES), q * TILE + k, jnp.int32)
            return jnp.take_along_axis(tile, where, axis=1, mode="promise_in_bounds")

        cols = [spread(piv[0], k) for k in range(TILE)]
        for t in range(TILE):
            inv = 1.0 / jnp.broadcast_to(cols[t][t:t + 1], (TILE, LANES))
            at = sub == t
            factor = jnp.where(at, 1.0 - inv, cols[t] * inv)
            cols = [c if k <= t else c - factor * jnp.broadcast_to(c[t:t + 1], (TILE, LANES)) for k, c in enumerate(cols)]
            piv = [c - factor * jnp.broadcast_to(c[t:t + 1], (TILE, LANES)) for c in piv]
        lines = [[jnp.broadcast_to(c[k:k + 1], (TILE, LANES)) for k in range(TILE)] for c in piv]
        for i in range(tiles):
            at = slice(first + i * TILE, first + (i + 1) * TILE)
            old = [mat[at, first + w * LANES:first + (w + 1) * LANES] for w in range(spans)]
            mult = [spread(old[0], k) for k in range(TILE)]
            for w in range(spans):
                acc = [mult[k] * lines[w][k] for k in range(TILE)]
                while len(acc) > 1:
                    acc = [acc[2 * z] + acc[2 * z + 1] for z in range(len(acc) // 2)]
                mat[at, first + w * LANES:first + (w + 1) * LANES] = old[w] - acc[0]
        for w in range(spans):
            mat[pl.ds(base, TILE), first + w * LANES:first + (w + 1) * LANES] = piv[w]
        return carry

    lax.fori_loop(0, tiles, group, 0)


def solver_kernel(jac_ref, resid_ref, weight_ref, prec_ref, mean_ref, state_ref, out_ref, aug, mat, held):
    count, size = jac_ref.shape
    rows, lanes = mat.shape
    root = jnp.sqrt(prec_ref[...])
    aug[...] = jnp.zeros_like(aug)
    jac = jac_ref[...] * (1.0 / root)
    aug[0:count, :] = jac
    aug[rows:rows + 1, :] = (state_ref[...] - mean_ref[...]) * root
    full = lax.dot_general(aug[0:rows, :], aug[...], (((1,), (1,)), ((), ())), precision=HI, preferred_element_type=jnp.float32)
    r = lax.broadcasted_iota(jnp.int32, full.shape, 0)
    c = lax.broadcasted_iota(jnp.int32, full.shape, 1)
    mat[...] = full + jnp.where(r == c, 1.0 / weight_ref[...], 0.0)
    for first in range(0, rows, LANES):
        here = min(LANES, rows - first)
        column = jnp.transpose(jnp.broadcast_to(resid_ref[:, first:first + LANES], (LANES, LANES)))[0:here, 0:1]
        mat[first:first + here, rows:rows + 1] = mat[first:first + here, rows:rows + 1] - column
    for first in range(0, rows, LANES):
        here = min(LANES, rows - first)
        after = first + here
        if after < rows:
            held[0:here, 0:lanes - after] = mat[first:after, after:lanes]
        eliminate(mat, first, here, lanes)
        if after < rows:
            mat[after:rows, after:lanes] = mat[after:rows, after:lanes] - lax.dot_general(
                held[0:here, 0:rows - after], mat[first:after, after:lanes], (((0,), (0,)), ((), ())),
                precision=HI, preferred_element_type=jnp.float32)
    out_ref[...] = back(mat, aug, rows, lanes, mean_ref, root)


def back(mat, aug, rows, lanes, mean_ref, root):
    total = None
    solved = []
    start = (rows - 1) // LANES * LANES
    for first in range(start, -1, -LANES):
        here = min(LANES, rows - first)
        z = mat[first:first + here, rows:rows + 1]
        for at, width, later in solved:
            z = z - jnp.sum(mat[first:first + here, at:at + width] * later, axis=1, keepdims=True)
        part = jnp.sum(aug[first:first + here, :] * z, axis=0, keepdims=True)
        total = part if total is None else total + part
        if first > 0:
            flat = jnp.transpose(jnp.broadcast_to(z, (here, LANES)))[0:1, :]
            solved.append((first, here, flat))
    return mean_ref[...] + total / root


def solve(states, resid, jac, weight, prec, mean):
    count, size = jac.shape
    rows = up(count, TILE)
    lanes = up(rows + 1, LANES)
    wide = lanes
    weight = jnp.pad(weight, (0, rows - count), constant_values=1.0)[:, None]
    resid = jnp.pad(resid, ((0, 0), (0, lanes - count)))
    vmem = pl.BlockSpec(memory_space=pltpu.VMEM)
    return pl.pallas_call(
        solver_kernel,
        out_shape=jax.ShapeDtypeStruct((1, size), jnp.float32),
        in_specs=[vmem] * 6,
        out_specs=vmem,
        scratch_shapes=[
            pltpu.VMEM((wide, size), jnp.float32),
            pltpu.VMEM((rows, lanes), jnp.float32),
            pltpu.VMEM((LANES, lanes), jnp.float32),
        ],
        compiler_params=pltpu.CompilerParams(vmem_limit_bytes=32 * 2**20),
    )(jac, resid, weight, prec[None, :], mean, states)


def partner(me, m, n):
    out, bit = 0, 1
    while bit < n:
        out = out + ((me // bit + (m // bit) % 2) % 2) * bit
        bit *= 2
    return out


def project_kernel(
    n, state_ref, jac_ref, eig_ref, valid_ref, base_ref, curve_ref, jac_out, resid_out,
    slabs, states, mis, weighted, sent, came, rows_out, rows_in,
    slab_sem, state_send, state_recv, jac_send, jac_recv, row_send, row_recv,
):
    me = lax.axis_index("chan")
    order = list(range(n - 1, 0, -1)) + [0]
    loads = {}
    for m in order:
        q = partner(me, m, n)
        loads[m] = pltpu.make_async_copy(jac_ref.at[q], slabs.at[m], slab_sem.at[m])
        loads[m].start()
    barrier = pltpu.get_barrier_semaphore()
    for m in range(1, n):
        pl.semaphore_signal(barrier, inc=1, device_id={"chan": partner(me, m, n)}, device_id_type=MESH)
    pl.semaphore_wait(barrier, n - 1)

    def send(src, dst, ssem, rsem, m):
        copy = pltpu.make_async_remote_copy(
            src_ref=src, dst_ref=dst, send_sem=ssem.at[m], recv_sem=rsem.at[m],
            device_id={"chan": partner(me, m, n)}, device_id_type=MESH)
        copy.start()
        return copy

    state_copies = {m: send(state_ref, states.at[m], state_send, state_recv, m) for m in range(1, n)}
    curve = curve_ref[...]
    row_copies, jac_copies = {}, {}
    for m in order:
        q = partner(me, m, n)
        if m:
            state_copies[m].wait_recv()
            state = states[m]
        else:
            state = state_ref[...]
        loads[m].wait()
        state = jnp.broadcast_to(state, (16, state.shape[1])).astype(jnp.bfloat16)
        linear = jnp.dot(state, slabs[m], preferred_element_type=jnp.float32)[0:8]
        valid = valid_ref[q]
        misfit = valid * (base_ref[q] + linear + 0.5 * curve * linear * linear)
        mis[m] = misfit[0:1]
        slope = valid * (1.0 + curve * linear)
        weighted[...] = (slope[0:1] * eig_ref[...].astype(jnp.float32)).astype(jnp.bfloat16)
        if m == 0:
            every = jnp.concatenate([mis[z] for z in range(n)] + [jnp.zeros_like(mis[0])] * (up(n, 16) - n), axis=0).astype(jnp.bfloat16)
            project = lax.dot_general(every, eig_ref[...], (((1,), (1,)), ((), ())), preferred_element_type=jnp.float32)
            for z in range(n):
                rows_out[z] = project[z:z + 1]
            for z in range(1, n):
                row_copies[z] = send(rows_out.at[z], rows_in.at[z], row_send, row_recv, z)
        part = lax.dot_general(weighted[...], slabs[m], (((1,), (1,)), ((), ())), preferred_element_type=jnp.float32)
        if m:
            sent[m] = part.astype(jnp.bfloat16)
            jac_copies[m] = send(sent.at[m], came.at[m], jac_send, jac_recv, m)
        else:
            jac_out[...] = part
    resid = rows_out[0]
    for m in order[:-1]:
        row_copies[m].wait_recv()
        resid = resid + rows_in[m]
    resid_out[...] = resid
    for m in order[:-1]:
        jac_copies[m].wait_recv()
        jac_out[...] += came[m].astype(jnp.float32)
    for m in range(1, n):
        state_copies[m].wait_send()
        row_copies[m].wait_send()
        jac_copies[m].wait_send()


def project(index, n, state, jac, eig, valid, base, curve):
    comps, chans = eig.shape
    size = jac.shape[1]
    vmem = pl.BlockSpec(memory_space=pltpu.VMEM)
    dma = pltpu.SemaphoreType.DMA((n,))
    return pl.pallas_call(
        functools.partial(project_kernel, n),
        out_shape=(jax.ShapeDtypeStruct((comps, size), jnp.float32), jax.ShapeDtypeStruct((1, comps), jnp.float32)),
        in_specs=[vmem, pl.BlockSpec(memory_space=pl.ANY), vmem, vmem, vmem, vmem],
        out_specs=(vmem, vmem),
        scratch_shapes=[
            pltpu.VMEM((n, size, chans), jnp.bfloat16),
            pltpu.VMEM((n, 1, size), jnp.float32),
            pltpu.VMEM((n, 1, chans), jnp.float32),
            pltpu.VMEM((comps, chans), jnp.bfloat16),
            pltpu.VMEM((n, comps, size), jnp.bfloat16),
            pltpu.VMEM((n, comps, size), jnp.bfloat16),
            pltpu.VMEM((n, 1, comps), jnp.float32),
            pltpu.VMEM((n, 1, comps), jnp.float32),
        ] + [dma] * 7,
        compiler_params=pltpu.CompilerParams(
            collective_id=index, has_side_effects=True, vmem_limit_bytes=48 * 2**20),
    )(state, jac, eig, valid, base, curve)


def local(
    observed,
    eigvec,
    jacobian,
    radiance_base,
    curvature,
    block_mask,
    pc_weight,
    prior_prec,
    prior_mean,
    state0,
    n,
):
    block_width = observed.shape[1] // block_mask.shape[1]
    states = state0
    valid = jnp.repeat(block_mask.astype(jnp.float32), block_width, axis=1)[:, None, :]
    base = (radiance_base.astype(jnp.float32)[None] - observed.astype(jnp.float32))[:, None, :]
    curve = curvature.astype(jnp.float32)[None]
    eig = eigvec.T
    jac = jnp.swapaxes(jacobian, 1, 2)
    for iteration in range(ITERS):
        pc_jacob, pc_resid = project(iteration, n, states, jac, eig, valid, base, curve)
        states = solve(states, pc_resid, pc_jacob, pc_weight, prior_prec, prior_mean)
    return states


def solution(mesh):
    return jax.shard_map(
        functools.partial(local, n=mesh.shape["chan"]),
        mesh=mesh,
        in_specs=(
            P("prof", "chan"),
            P("chan", None),
            P("prof", "chan", None),
            P("chan"),
            P("chan"),
            P("prof", "chan"),
            P(),
            P(),
            P(("prof", "chan"), None),
            P(("prof", "chan"), None),
        ),
        out_specs=P(("prof", "chan"), None),
        check_vma=False,
    )
```

```python
import functools
import jax, jax.numpy as jnp
from jax import lax
from jax.experimental import pallas as pl
from jax.experimental.pallas import tpu as pltpu

from jax.sharding import PartitionSpec as P

ITERS = 2
TILE, LANES = 8, 128
BLOCK = 32
MESH = pl.DeviceIdType.MESH


def up(n, m):
    return -(-n // m) * m


def split(x):
    high = x.astype(jnp.bfloat16)
    return high, (x - high.astype(jnp.float32)).astype(jnp.bfloat16)


def product(a, b, dims):
    (ah, al), (bh, bl) = split(a), split(b)
    dot = functools.partial(lax.dot_general, dimension_numbers=(dims, ((), ())), preferred_element_type=jnp.float32)
    return dot(ah, bh) + (dot(ah, bl) + dot(al, bh))


def eliminate(mat, first, rows, width):
    tiles = rows // TILE
    left = first // LANES * LANES
    spans = (width - left) // LANES
    sub = lax.broadcasted_iota(jnp.int32, (TILE, LANES), 0)

    def group(q, carry):
        base = pl.multiple_of(first + q * TILE, TILE)
        piv = [mat[pl.ds(base, TILE), left + w * LANES:left + (w + 1) * LANES] for w in range(spans)]

        def spread(tile, k):
            where = jnp.full((TILE, LANES), first - left + q * TILE + k, jnp.int32)
            return jnp.take_along_axis(tile, where, axis=1, mode="promise_in_bounds")

        cols = [spread(piv[0], k) for k in range(TILE)]
        for t in range(TILE):
            inv = 1.0 / jnp.broadcast_to(cols[t][t:t + 1], (TILE, LANES))
            at = sub == t
            factor = jnp.where(at, 1.0 - inv, cols[t] * inv)
            cols = [c if k <= t else c - factor * jnp.broadcast_to(c[t:t + 1], (TILE, LANES)) for k, c in enumerate(cols)]
            piv = [c - factor * jnp.broadcast_to(c[t:t + 1], (TILE, LANES)) for c in piv]
        lines = [[jnp.broadcast_to(c[k:k + 1], (TILE, LANES)) for k in range(TILE)] for c in piv]
        for i in range(tiles):
            at = slice(first + i * TILE, first + (i + 1) * TILE)
            old = [mat[at, left + w * LANES:left + (w + 1) * LANES] for w in range(spans)]
            mult = [spread(old[0], k) for k in range(TILE)]
            for w in range(spans):
                acc = [mult[k] * lines[w][k] for k in range(TILE)]
                while len(acc) > 1:
                    acc = [acc[2 * z] + acc[2 * z + 1] for z in range(len(acc) // 2)]
                mat[at, left + w * LANES:left + (w + 1) * LANES] = old[w] - acc[0]
        for w in range(spans):
            mat[pl.ds(base, TILE), left + w * LANES:left + (w + 1) * LANES] = piv[w]
        return carry

    lax.fori_loop(0, tiles, group, 0)


def solver_kernel(jac_ref, resid_ref, weight_ref, prec_ref, mean_ref, state_ref, out_ref, aug, mat, held):
    count, size = jac_ref.shape
    rows, lanes = mat.shape
    root = jnp.sqrt(prec_ref[...])
    aug[...] = jnp.zeros_like(aug)
    jac = jac_ref[...] * (1.0 / root)
    aug[0:count, :] = jac
    aug[rows:rows + 1, :] = (state_ref[...] - mean_ref[...]) * root
    full = product(aug[0:rows, :], aug[...], ((1,), (1,)))
    r = lax.broadcasted_iota(jnp.int32, full.shape, 0)
    c = lax.broadcasted_iota(jnp.int32, full.shape, 1)
    mat[...] = full + jnp.where(r == c, 1.0 / weight_ref[...], 0.0)
    for first in range(0, rows, LANES):
        here = min(LANES, rows - first)
        column = jnp.transpose(jnp.broadcast_to(resid_ref[:, first:first + LANES], (LANES, LANES)))[0:here, 0:1]
        mat[first:first + here, rows:rows + 1] = mat[first:first + here, rows:rows + 1] - column
    for first in range(0, rows, BLOCK):
        here = min(BLOCK, rows - first)
        after = first + here
        left = after // LANES * LANES
        if after < rows:
            held[0:here, 0:lanes - left] = mat[first:after, left:lanes]
        eliminate(mat, first, here, lanes)
        if after < rows:
            change = product(held[0:here, 0:rows - left], mat[first:after, left:lanes], ((0,), (0,)))
            mat[after:rows, left:lanes] = mat[after:rows, left:lanes] - change[after - left:]
    out_ref[...] = back(mat, aug, rows, lanes, mean_ref, root)


def back(mat, aug, rows, lanes, mean_ref, root):
    total = None
    solved = jnp.zeros((1, lanes), jnp.float32)
    for first in range((rows - 1) // BLOCK * BLOCK, -1, -BLOCK):
        here = min(BLOCK, rows - first)
        z = mat[first:first + here, rows:rows + 1] - jnp.sum(mat[first:first + here, :] * solved, axis=1, keepdims=True)
        part = jnp.sum(aug[first:first + here, :] * z, axis=0, keepdims=True)
        total = part if total is None else total + part
        r = lax.broadcasted_iota(jnp.int32, (here, lanes), 0)
        c = lax.broadcasted_iota(jnp.int32, (here, lanes), 1)
        solved = solved + jnp.sum(jnp.where(r + first == c, z, 0.0), axis=0, keepdims=True)
    return mean_ref[...] + total / root


def solve(states, resid, jac, weight, prec, mean):
    count, size = jac.shape
    rows = up(count, TILE)
    lanes = up(rows + 1, LANES)
    wide = lanes
    weight = jnp.pad(weight, (0, rows - count), constant_values=1.0)[:, None]
    resid = jnp.pad(resid, ((0, 0), (0, lanes - count)))
    vmem = pl.BlockSpec(memory_space=pltpu.VMEM)
    return pl.pallas_call(
        solver_kernel,
        out_shape=jax.ShapeDtypeStruct((1, size), jnp.float32),
        in_specs=[vmem] * 6,
        out_specs=vmem,
        scratch_shapes=[
            pltpu.VMEM((wide, size), jnp.float32),
            pltpu.VMEM((rows, lanes), jnp.float32),
            pltpu.VMEM((LANES, lanes), jnp.float32),
        ],
        compiler_params=pltpu.CompilerParams(vmem_limit_bytes=32 * 2**20),
    )(jac, resid, weight, prec[None, :], mean, states)


def partner(me, m, n):
    out, bit = 0, 1
    while bit < n:
        out = out + ((me // bit + (m // bit) % 2) % 2) * bit
        bit *= 2
    return out


def project_kernel(
    n, state_ref, jac_ref, eig_ref, valid_ref, base_ref, curve_ref, jac_out, resid_out,
    slabs, states, mis, weighted, sent, came, rows_out, rows_in,
    slab_sem, state_send, state_recv, jac_send, jac_recv, row_send, row_recv,
):
    me = lax.axis_index("chan")
    order = list(range(n - 1, 0, -1)) + [0]
    loads = {}
    for m in order:
        q = partner(me, m, n)
        loads[m] = pltpu.make_async_copy(jac_ref.at[q], slabs.at[m], slab_sem.at[m])
        loads[m].start()
    barrier = pltpu.get_barrier_semaphore()
    for m in range(1, n):
        pl.semaphore_signal(barrier, inc=1, device_id={"chan": partner(me, m, n)}, device_id_type=MESH)
    pl.semaphore_wait(barrier, n - 1)

    def send(src, dst, ssem, rsem, m):
        copy = pltpu.make_async_remote_copy(
            src_ref=src, dst_ref=dst, send_sem=ssem.at[m], recv_sem=rsem.at[m],
            device_id={"chan": partner(me, m, n)}, device_id_type=MESH)
        copy.start()
        return copy

    state_copies = {m: send(state_ref, states.at[m], state_send, state_recv, m) for m in range(1, n)}
    curve = curve_ref[...]
    row_copies, jac_copies = {}, {}
    for m in order:
        q = partner(me, m, n)
        if m:
            state_copies[m].wait_recv()
            state = states[m]
        else:
            state = state_ref[...]
        loads[m].wait()
        state = jnp.broadcast_to(state, (16, state.shape[1])).astype(jnp.bfloat16)
        linear = jnp.dot(state, slabs[m], preferred_element_type=jnp.float32)[0:8]
        valid = valid_ref[q]
        misfit = valid * (base_ref[q] + linear + 0.5 * curve * linear * linear)
        mis[m] = misfit[0:1]
        slope = valid * (1.0 + curve * linear)
        weighted[...] = (slope[0:1] * eig_ref[...].astype(jnp.float32)).astype(jnp.bfloat16)
        if m == 0:
            every = jnp.concatenate([mis[z] for z in range(n)] + [jnp.zeros_like(mis[0])] * (up(n, 16) - n), axis=0).astype(jnp.bfloat16)
            project = lax.dot_general(every, eig_ref[...], (((1,), (1,)), ((), ())), preferred_element_type=jnp.float32)
            for z in range(n):
                rows_out[z] = project[z:z + 1]
            for z in range(1, n):
                row_copies[z] = send(rows_out.at[z], rows_in.at[z], row_send, row_recv, z)
        part = lax.dot_general(weighted[...], slabs[m], (((1,), (1,)), ((), ())), preferred_element_type=jnp.float32)
        if m:
            sent[m] = part.astype(jnp.bfloat16)
            jac_copies[m] = send(sent.at[m], came.at[m], jac_send, jac_recv, m)
        else:
            jac_out[...] = part
    resid = rows_out[0]
    for m in order[:-1]:
        row_copies[m].wait_recv()
        resid = resid + rows_in[m]
    resid_out[...] = resid
    for m in order[:-1]:
        jac_copies[m].wait_recv()
        jac_out[...] += came[m].astype(jnp.float32)
    for m in range(1, n):
        state_copies[m].wait_send()
        row_copies[m].wait_send()
        jac_copies[m].wait_send()


def project(index, n, state, jac, eig, valid, base, curve):
    comps, chans = eig.shape
    size = jac.shape[1]
    vmem = pl.BlockSpec(memory_space=pltpu.VMEM)
    dma = pltpu.SemaphoreType.DMA((n,))
    return pl.pallas_call(
        functools.partial(project_kernel, n),
        out_shape=(jax.ShapeDtypeStruct((comps, size), jnp.float32), jax.ShapeDtypeStruct((1, comps), jnp.float32)),
        in_specs=[vmem, pl.BlockSpec(memory_space=pl.ANY), vmem, vmem, vmem, vmem],
        out_specs=(vmem, vmem),
        scratch_shapes=[
            pltpu.VMEM((n, size, chans), jnp.bfloat16),
            pltpu.VMEM((n, 1, size), jnp.float32),
            pltpu.VMEM((n, 1, chans), jnp.float32),
            pltpu.VMEM((comps, chans), jnp.bfloat16),
            pltpu.VMEM((n, comps, size), jnp.bfloat16),
            pltpu.VMEM((n, comps, size), jnp.bfloat16),
            pltpu.VMEM((n, 1, comps), jnp.float32),
            pltpu.VMEM((n, 1, comps), jnp.float32),
        ] + [dma] * 7,
        compiler_params=pltpu.CompilerParams(
            collective_id=index, has_side_effects=True, vmem_limit_bytes=48 * 2**20),
    )(state, jac, eig, valid, base, curve)


def local(
    observed,
    eigvec,
    jacobian,
    radiance_base,
    curvature,
    block_mask,
    pc_weight,
    prior_prec,
    prior_mean,
    state0,
    n,
):
    block_width = observed.shape[1] // block_mask.shape[1]
    states = state0
    valid = jnp.repeat(block_mask.astype(jnp.float32), block_width, axis=1)[:, None, :]
    base = (radiance_base.astype(jnp.float32)[None] - observed.astype(jnp.float32))[:, None, :]
    curve = curvature.astype(jnp.float32)[None]
    eig = eigvec.T
    jac = jnp.swapaxes(jacobian, 1, 2)
    for iteration in range(ITERS):
        pc_jacob, pc_resid = project(iteration, n, states, jac, eig, valid, base, curve)
        states = solve(states, pc_resid, pc_jacob, pc_weight, prior_prec, prior_mean)
    return states


def solution(mesh):
    return jax.shard_map(
        functools.partial(local, n=mesh.shape["chan"]),
        mesh=mesh,
        in_specs=(
            P("prof", "chan"),
            P("chan", None),
            P("prof", "chan", None),
            P("chan"),
            P("chan"),
            P("prof", "chan"),
            P(),
            P(),
            P(("prof", "chan"), None),
            P(("prof", "chan"), None),
        ),
        out_specs=P(("prof", "chan"), None),
        check_vma=False,
    )
```
